32 devices in a mesh: row: 4 (over y, x), col: 8 (over z, core).
Axes of the slice: x: 2, y: 2, z: 4, core: 2. Of those that a mesh axis runs over, the one named last changes fastest.
Arguments:
- features: bfloat16 [8192, 128], P(('row', 'col')), may hold values from -6 to 6
- weight: bfloat16 [128, 256], replicated, may hold values from -0.5 to 0.5
- cotangent: bfloat16 [8192, 256], P(('row', 'col')), may hold values from -6 to 6
- tile_values: bfloat16 [4, 8, 96, 128, 128], P('row', 'col'), may hold values from -0.3125 to 0.3125
- tile_rows: int32 [4, 8, 96], P('row', 'col'), may hold values from 0 to 15
- tile_cols: int32 [4, 8, 96], P('row', 'col'), may hold values from 0 to 7
- tile_counts: int32 [4, 8], P('row', 'col'), may hold values from 12 to 96, as said below
Outputs:
- output: bfloat16 [8192, 256], P(('row', 'col'))
- grad_features: bfloat16 [8192, 128], P(('row', 'col'))
- grad_weight: float32 [128, 256], replicated
The draws below stay inside these ranges and needn't reach their ends.
Inputs may be any that keep to these rules, and one draw needn't show every extreme that they name: Slots 0 to tile_counts - 1 of a grid cell are live and the rest are ignored; the (row tile, column tile) pairs of a cell's live slots are distinct; some cells hold 96 live slots.
All inputs are finite; a program needn't handle non-finite values.
Results may differ from the reference program's by a relative error of at most 0.0049.
Values may be sent and summed in bfloat16 or wider, within the bound.
A program may use at most 128 MiB of HBM per device.

```python
import jax
import jax.numpy as jnp
from jax import lax

F = 128
H = 256
TILE = 128
NB = 256
GRID_ROWS = 4
GRID_COLS = 8
NODES = 8192
RT = 16
CT = 8
TMAX = 96


def tile_slots(key):
    folded = jax.random.fold_in(key, 7)
    device_keys = jax.random.split(folded, GRID_ROWS * GRID_COLS)

    def one_device(device_key):
        return jax.random.permutation(device_key, RT * CT)[:TMAX]
    slot_ids = jax.vmap(one_device)(device_keys)
    return slot_ids.reshape(GRID_ROWS, GRID_COLS, TMAX).astype(jnp.int32)


def draw_tile_rows(key, part):
    return tile_slots(key) // CT


def draw_tile_cols(key, part):
    return tile_slots(key) % CT


def draw_tile_counts(key, part):
    folded = jax.random.fold_in(key, 11)
    key_counts, key_heavy = jax.random.split(folded)
    counts = jax.random.randint(key_counts, (GRID_ROWS * GRID_COLS,), TMAX // 8, TMAX // 2 + 1)
    heavy_ids = jax.random.permutation(key_heavy, GRID_ROWS * GRID_COLS)[:4]
    counts = counts.at[heavy_ids].set(TMAX)
    return counts.reshape(GRID_ROWS, GRID_COLS).astype(jnp.int32)


def shard_levels(own_key, dims, cuts, smallest, top_value):
    factor_of, own = 1.0, jax.random.fold_in(own_key, 6)
    for axis_at, blocks in cuts:
        heights = jnp.exp(jax.random.uniform(jax.random.fold_in(own, axis_at), (blocks,), jnp.float32, smallest / len(cuts), top_value / len(cuts)))
        factor_of = factor_of * jnp.repeat(heights, dims[axis_at] // blocks).reshape([-1 if axis == axis_at else 1 for axis in range(len(dims))])
    return factor_of


def normal_values(own_key, dims, scale, bound, pieces=(), dtype=jnp.bfloat16):
    entries = scale * jax.random.normal(own_key, dims, jnp.float32)
    if pieces:
        entries = entries * shard_levels(own_key, dims, pieces, -0.22, 0.18)
    return jnp.clip(entries, -bound, bound).astype(dtype)


def setup_inputs(seed: int = 0) -> dict:
    keys = jax.random.split(jax.random.key(seed), 8)
    features = normal_values(keys[0], (NODES, F), 1.0, 6.0, ((0, 32),))
    weight = normal_values(keys[1], (F, H), F ** -0.5, 0.5)
    cotangent = normal_values(keys[2], (NODES, H), 1.0, 6.0, ((0, 32),))
    tile_values = normal_values(keys[3], (GRID_ROWS, GRID_COLS, TMAX, TILE, TILE), ((5 * TILE * GRID_COLS * TMAX / (16 * RT)) ** -0.5), 0.3125, ((0, 4), (1, 8)))
    tile_rows = draw_tile_rows(jax.random.fold_in(keys[7], 71), 0)
    tile_cols = draw_tile_cols(jax.random.fold_in(keys[7], 71), 0)
    tile_counts = draw_tile_counts(jax.random.fold_in(keys[7], 71), 0)
    return {"features": features, "weight": weight, "cotangent": cotangent, "tile_values": tile_values, "tile_rows": tile_rows, "tile_cols": tile_cols, "tile_counts": tile_counts}


def silu_slope(values):
    sigmoid_part = jax.nn.sigmoid(values)
    return sigmoid_part * (1.0 + values * (1.0 - sigmoid_part))


def tile_product(slot_values, slot_rows, slot_cols, live_count, source, out_tiles):
    live_mask = jnp.arange(slot_values.shape[0]) < live_count
    weights = jnp.where(live_mask[:, None, None], slot_values.astype(jnp.float32), jnp.zeros((), jnp.float32))
    picked = jnp.take(source, slot_cols, axis=0).astype(jnp.float32)
    products = jnp.einsum('tij,tjh->tih', weights, picked, precision=lax.Precision.HIGHEST)
    empty = jnp.zeros((out_tiles,) + products.shape[1:], jnp.float32)
    return empty.at[slot_rows].add(products)


def reference(features, weight, cotangent, tile_values, tile_rows, tile_cols, tile_counts):
    blocks = features.reshape(GRID_ROWS, GRID_COLS, NB, F)
    sources = jnp.swapaxes(blocks, 0, 1).reshape(GRID_COLS, CT, TILE, F)

    def forward_row(row_args):
        def add_block(running, block_args):
            block_values, block_rows, block_cols, block_count, block_source = block_args
            return running + tile_product(block_values, block_rows, block_cols, block_count, block_source, RT), None

        running, unused = lax.scan(add_block, jnp.zeros((RT, TILE, F), jnp.float32), tuple(row_args) + (sources,))
        return running

    aggregated = lax.map(forward_row, (tile_values, tile_rows, tile_cols, tile_counts)).reshape(NODES, F)
    summed = jnp.dot(aggregated, weight.astype(jnp.float32), precision=lax.Precision.HIGHEST)
    output = jax.nn.silu(summed).astype(jnp.bfloat16)
    grad_summed = (cotangent.astype(jnp.float32) * silu_slope(summed)).astype(jnp.bfloat16)
    grad_sources = grad_summed.reshape(GRID_ROWS, RT, TILE, H)

    def backward_col(col_index):
        def add_block(running, row_index):
            flipped = jnp.swapaxes(tile_values[row_index, col_index], 1, 2)
            term = tile_product(flipped, tile_cols[row_index, col_index], tile_rows[row_index, col_index], tile_counts[row_index, col_index], grad_sources[row_index], CT)
            return running + term, None

        running, unused = lax.scan(add_block, jnp.zeros((CT, TILE, H), jnp.float32), jnp.arange(GRID_ROWS))
        return running

    grad_cols = lax.map(backward_col, jnp.arange(GRID_COLS))
    grad_mixed = jnp.swapaxes(grad_cols.reshape(GRID_COLS, GRID_ROWS, NB, H), 0, 1).reshape(NODES, H)
    grad_features = jnp.dot(grad_mixed, weight.astype(jnp.float32).T, precision=lax.Precision.HIGHEST).astype(jnp.bfloat16)
    grad_weight = jnp.dot(features.astype(jnp.float32).T, grad_mixed, precision=lax.Precision.HIGHEST) * (NODES ** -0.5)
    return output, grad_features, grad_weight
```

```python
import functools

import jax
import jax.numpy as jnp
from jax import lax
from jax.experimental import pallas as pl
from jax.experimental.pallas import tpu as pltpu
from jax.sharding import PartitionSpec as P

MESH = pl.DeviceIdType.MESH
PARTS = 2


def dot_nn(a, b):
    return lax.dot_general(a, b, (((1,), (0,)), ((), ())), preferred_element_type=jnp.float32)


def dot_nt(a, b):
    return lax.dot_general(a, b, (((1,), (1,)), ((), ())), preferred_element_type=jnp.float32)


def split_high_low(values):
    high = values.astype(jnp.bfloat16)
    return high, (values - high.astype(jnp.float32)).astype(jnp.bfloat16)


def finish(*refs):
    count = len(refs) // 2
    sems = refs[-1]
    copies = [pltpu.make_async_copy(refs[k], refs[count + k], sems.at[k]) for k in range(count)]
    for copy in copies:
        copy.start()
    for copy in copies:
        copy.wait()


def partner_index(index, step, count):
    if count & (count - 1):
        return lax.rem(count + step - index, count)
    paired, bit = index, 1
    while bit <= step:
        if step & bit:
            paired = paired + bit - 2 * bit * ((index // bit) % 2)
        bit *= 2
    return paired


def each(count, body):
    if count <= 8:
        for index in range(count):
            body(index)
    else:
        lax.fori_loop(0, count, lambda index, carry: (body(index), carry)[1], 0)


def kernel(rows, cols, sizes, live_hbm, row_hbm, col_hbm, feats_hbm, weight_hbm, cot_hbm, tiles_hbm,
           out, grad_feat, grad_weight,
           live, tile_row, tile_col, feats, weight, cot, keys, table, slot_of, slots, dense, weight_t, cot_t,
           feat_all, part, pair_send, pair_recv, own_sum, hop_send, hop_recv, grad_all, acc, row_send, row_recv,
           w_term, w_row, w_quarter, w_pair, w_hop, w_all,
           load_sem, feat_s, feat_r, pair_s, pair_r, hop_s, hop_r, gp_s, gp_r, gz_s, gz_r, gf_s, gf_r,
           row_s, row_r, w1_s, w1_r, w2_s, w2_r, w3_s, w3_r, w4_s, w4_r, w5_s, w5_r):
    block, tile, row_tiles, col_tiles, slot_total = sizes
    chips = cols // 2
    width = feats.shape[1]
    piece = width // PARTS
    i = lax.axis_index("row")
    j = lax.axis_index("col")
    q = j // 2
    core = j % 2
    other = 1 - core
    partner = (i, 2 * q + other)
    f32, bf16 = jnp.float32, jnp.bfloat16

    def row_at(step):
        return partner_index(i, step, rows)

    def chip_at(step):
        return partner_index(q, step, chips)

    def row_peer(step):
        return (row_at(step), j)

    def chip_peer(step):
        return (i, 2 * chip_at(step) + core)

    started = []

    def send(src, dst, ssem, rsem, device):
        copy = pltpu.make_async_remote_copy(
            src_ref=src, dst_ref=dst, send_sem=ssem, recv_sem=rsem, device_id=device, device_id_type=MESH)
        copy.start()
        started.append(copy)
        return copy

    barrier = pltpu.get_barrier_semaphore()
    peers = [partner] + [row_peer(d) for d in range(1, rows)] + [chip_peer(d) for d in range(1, chips)]
    for peer in peers:
        pl.semaphore_signal(barrier, inc=1, device_id=peer, device_id_type=MESH)

    loads = []
    for k, (src, dst) in enumerate((
            (live_hbm, live), (row_hbm, tile_row), (col_hbm, tile_col), (feats_hbm, feats),
            (tiles_hbm, slots.at[pl.ds(0, slot_total)]), (weight_hbm, weight), (cot_hbm, cot))):
        loads.append(pltpu.make_async_copy(src, dst, load_sem.at[k]))
        loads[-1].start()
    slots[slot_total] = jnp.zeros((tile, tile), bf16)
    keys[...] = jnp.full(keys.shape, -1, jnp.int32)

    for copy in loads[:3]:
        copy.wait()
    cell_total = row_tiles * col_tiles
    lanes = lax.broadcasted_iota(jnp.int32, (1, slot_total), 1)
    keys[:, :slot_total] = jnp.where(lanes < live[...], tile_row[...] * col_tiles + tile_col[...], -1)
    padded = keys.shape[1]
    key_columns = jnp.broadcast_to(keys[...], (128, padded)).T
    slot_ids = lax.broadcasted_iota(jnp.int32, (padded, 128), 0) - slot_total
    cell_ids = lax.broadcasted_iota(jnp.int32, (padded, 128), 1)
    for first in range(0, cell_total, 128):
        found = jnp.where(key_columns == cell_ids + first, slot_ids, 0)
        table[:, first:first + 128] = jnp.sum(found, axis=0, keepdims=True) + slot_total
    load_table = pltpu.make_async_copy(table, slot_of, load_sem.at[7])
    load_table.start()

    loads[3].wait()
    turned = feats[...].astype(f32).T.astype(bf16)
    for h in range(PARTS):
        feat_all[h, i] = turned[h * piece:(h + 1) * piece]

    pl.semaphore_wait(barrier, len(peers))

    feat_copies = {}
    for h in range(PARTS):
        for d in range(rows - 1, 0, -1):
            k = h * (rows - 1) + d - 1
            feat_copies[h, d] = send(feat_all.at[h, i], feat_all.at[h, i], feat_s.at[k], feat_r.at[k], row_peer(d))

    load_table.wait()
    loads[4].wait()

    def place(r, carry):
        at = pl.ds(pl.multiple_of(r * tile, tile), tile)
        for c in range(col_tiles):
            dense[at, c * tile:(c + 1) * tile] = slots[slot_of[0, r * col_tiles + c]]
        return carry

    lax.fori_loop(0, row_tiles, place, 0)

    def block_at(index):
        if isinstance(index, int):
            return pl.ds(index * block, block)
        return pl.ds(pl.multiple_of(index * block, block), block)

    def lines(h):
        return pl.ds(h * piece, piece)

    def forward_term(h, dest, source):
        return dot_nt(feat_all[h, source], dense[block_at(dest), block_at(source)])

    own_turned = jnp.concatenate([feat_all[h, i] for h in range(PARTS)], axis=0)

    def add_own(dest):
        part[dest] = dot_nt(own_turned, dense[block_at(dest), block_at(i)])

    each(cols, add_own)

    loads[5].wait()
    loads[6].wait()
    weight_t[...] = weight[...].astype(f32).T.astype(bf16)
    cot_t[...] = cot[...].astype(f32).T

    def add_sources(h):
        for d in range(1, rows - 1):
            feat_copies[h, d].wait_recv()
            source = row_at(d)

            def add_source(dest):
                part[dest, lines(h)] += forward_term(h, dest, source)

            each(cols, add_source)

    order = list(range(chips - 1, -1, -1))
    pair_copies = {}

    def last_source(h):
        feat_copies[h, rows - 1].wait_recv()
        source = row_at(rows - 1)
        for d in order:
            dest = 2 * chip_at(d) + other
            pair_send[h, d] = (part[dest, lines(h)] + forward_term(h, dest, source)).astype(bf16)
        pair_copies[h] = send(pair_send.at[h], pair_recv.at[h], pair_s.at[h], pair_r.at[h], partner)
        for d in order:
            dest = 2 * chip_at(d) + core
            part[dest, lines(h)] += forward_term(h, dest, source)

    hop_copies = {}

    def send_hops(h):
        pair_copies[h].wait_recv()
        for d in order:
            mine = part[2 * chip_at(d) + core, lines(h)] + pair_recv[h, d].astype(f32)
            if d:
                k = h * (chips - 1) + d - 1
                hop_send[h, d - 1] = mine.astype(bf16)
                hop_copies[h, d] = send(hop_send.at[h, d - 1], hop_recv.at[h, d - 1], hop_s.at[k], hop_r.at[k],
                                        chip_peer(d))
            else:
                own_sum[h] = mine

    add_sources(0)
    last_source(0)
    for h in range(1, PARTS):
        add_sources(h)
        send_hops(h - 1)
        last_source(h)
    send_hops(PARTS - 1)

    mixed = []
    for h in range(PARTS):
        total = own_sum[h]
        for d in range(1, chips):
            hop_copies[h, d].wait_recv()
            total = total + hop_recv[h, d - 1].astype(f32)
        mixed.append(total)
    high, low = split_high_low(jnp.concatenate(mixed, axis=0))
    summed = dot_nn(weight_t[...], high) + dot_nn(weight_t[...], low)
    gate = 1.0 / (1.0 + jnp.exp(-summed))
    slope = gate * (1.0 + summed * (1.0 - gate))
    grad = (cot_t[...] * slope).astype(bf16)
    back = dot_nn(weight[...], grad).astype(bf16)
    for h in range(PARTS):
        grad_all[j, h] = back[h * piece:(h + 1) * piece]
    gz_copies = {}
    for h in range(PARTS):
        for d in order[:-1]:
            k = h * (chips - 1) + d - 1
            gz_copies[h, d] = send(grad_all.at[j, h], grad_all.at[j, h], gz_s.at[k], gz_r.at[k], chip_peer(d))
    gp_copy = send(grad_all.at[j], grad_all.at[j], gp_s.at[0], gp_r.at[0], partner)

    scale = float(rows * cols * block) ** -0.5
    w_term[...] = (dot_nt(high, grad) + dot_nt(low, grad)) * scale
    quarter = width // rows
    half = quarter // 2

    def quarter_at(index):
        return pl.ds(pl.multiple_of(index * quarter, quarter), quarter)

    w1_copies = []
    for d in range(1, rows):
        w1_copies.append(send(w_term.at[quarter_at(row_at(d))], w_row.at[d - 1], w1_s.at[d - 1], w1_r.at[d - 1],
                              row_peer(d)))

    out[...] = (summed * gate).T.astype(out.dtype)

    def add_whole(source, first):
        grads = jnp.concatenate([grad_all[source, h] for h in range(PARTS)], axis=0)
        for r in range(rows):
            term = dot_nn(grads, dense[block_at(source), r * block:(r + 1) * block])
            if first:
                acc[r] = term
            else:
                acc[r] += term

    def add_part(source, h):
        for r in range(rows):
            acc[r, lines(h)] += dot_nn(grad_all[source, h], dense[block_at(source), r * block:(r + 1) * block])

    add_whole(j, True)
    gp_copy.wait_recv()
    add_whole(2 * q + other, False)

    gf_copies = {}

    def arrive(h, d):
        gz_copies[h, d].wait_recv()
        source = 2 * chip_at(d) + core
        k = h * (chips - 1) + d - 1
        gf_copies[h, d] = send(grad_all.at[source, h], grad_all.at[source, h], gf_s.at[k], gf_r.at[k], partner)
        add_part(source, h)

    def passed(h, d):
        gf_copies[h, d].wait_recv()
        add_part(2 * chip_at(d) + other, h)

    row_copies = {}

    def send_rows(h):
        for d in range(rows - 1, 0, -1):
            k = h * (rows - 1) + d - 1
            row_send[h, d - 1] = acc[row_at(d), lines(h)].astype(bf16)
            row_copies[h, d] = send(row_send.at[h, d - 1], row_recv.at[h, d - 1], row_s.at[k], row_r.at[k],
                                    row_peer(d))

    w2_copies = []
    w3_copies = []

    def second_weight_step():
        total = w_term[quarter_at(i)]
        for d, copy in enumerate(w1_copies):
            copy.wait_recv()
            total = total + w_row[d]
        w_quarter[...] = total
        w2_copies.append(send(w_quarter.at[pl.ds(pl.multiple_of(other * half, half), half)], w_pair, w2_s.at[0],
                              w2_r.at[0], partner))

    def third_weight_step():
        w2_copies[0].wait_recv()
        w_hop[q] = w_quarter[pl.ds(pl.multiple_of(core * half, half), half)] + w_pair[...]
        for d in range(1, chips):
            w3_copies.append(send(w_hop.at[q], w_hop.at[q], w3_s.at[d - 1], w3_r.at[d - 1], chip_peer(d)))

    arrivals = [(h, d) for h in range(PARTS) for d in range(1, chips)]
    for at, (h, d) in enumerate(arrivals):
        arrive(h, d)
        if at == 1:
            second_weight_step()
        if at == chips - 1:
            third_weight_step()
        if at:
            before = arrivals[at - 1]
            passed(*before)
            if before[1] == chips - 1:
                send_rows(before[0])
    passed(*arrivals[-1])
    send_rows(PARTS - 1)

    for copy in w3_copies:
        copy.wait_recv()
    total = w_hop[0]
    for k in range(1, chips):
        total = total + w_hop[k]
    w_all[core, i] = total
    w4_copies = []
    for d in range(1, rows):
        w4_copies.append(send(w_all.at[core, i], w_all.at[core, i], w4_s.at[d - 1], w4_r.at[d - 1], row_peer(d)))

    finals = []
    for h in range(PARTS):
        final = acc[i, lines(h)]
        for d in range(1, rows):
            row_copies[h, d].wait_recv()
            final = final + row_recv[h, d - 1].astype(f32)
        finals.append(final)
    grad_feat[...] = jnp.concatenate(finals, axis=0).T.astype(grad_feat.dtype)
    for copy in w4_copies:
        copy.wait_recv()
    w5_copy = send(w_all.at[core], w_all.at[core], w5_s.at[0], w5_r.at[0], partner)
    w5_copy.wait_recv()
    for r in range(rows):
        for c in range(2):
            at = (2 * r + c) * half
            grad_weight[at:at + half] = w_all[c, r]
    for copy in started:
        copy.wait_send()


def local(features, weight, cotangent, tile_values, tile_rows, tile_cols, tile_counts):
    rows = lax.axis_size("row")
    cols = lax.axis_size("col")
    chips = cols // 2
    block, width = features.shape
    hidden = weight.shape[1]
    slot_total, tile = tile_values.shape[2], tile_values.shape[3]
    row_tiles = cols * block // tile
    col_tiles = rows * block // tile
    cell_total = row_tiles * col_tiles
    half = width // rows // 2
    piece = width // PARTS
    bf16, f32, i32 = jnp.bfloat16, jnp.float32, jnp.int32
    dma = pltpu.SemaphoreType.DMA
    v = pltpu.VMEM
    sizes = (block, tile, row_tiles, col_tiles, slot_total)
    scratch = [
        v((1, 1), i32),
        v((1, slot_total), i32),
        v((1, slot_total), i32),
        v((block, width), bf16),
        v((width, hidden), bf16),
        v((block, hidden), bf16),
        v((1, pl.cdiv(slot_total, 128) * 128), i32),
        v((1, cell_total), i32),
        pltpu.SMEM((1, cell_total), i32),
        v((slot_total + 1, tile, tile), bf16),
        v((row_tiles * tile, col_tiles * tile), bf16),
        v((hidden, width), bf16),
        v((hidden, block), f32),
        v((PARTS, rows, piece, block), bf16),
        v((cols, width, block), f32),
        v((PARTS, chips, piece, block), bf16),
        v((PARTS, chips, piece, block), bf16),
        v((PARTS, piece, block), f32),
        v((PARTS, chips - 1, piece, block), bf16),
        v((PARTS, chips - 1, piece, block), bf16),
        v((cols, PARTS, piece, block), bf16),
        v((rows, width, block), f32),
        v((PARTS, rows - 1, piece, block), bf16),
        v((PARTS, rows - 1, piece, block), bf16),
        v((width, hidden), f32),
        v((rows - 1, 2 * half, hidden), f32),
        v((2 * half, hidden), f32),
        v((half, hidden), f32),
        v((chips, half, hidden), f32),
        v((2, rows, half, hidden), f32),
        dma((8,)),
    ]
    for count in (PARTS * (rows - 1), PARTS, PARTS * (chips - 1), 1, PARTS * (chips - 1), PARTS * (chips - 1),
                  PARTS * (rows - 1), rows - 1, 1, chips - 1, rows - 1, 1):
        scratch += [dma((count,)), dma((count,))]
    vmem = pl.BlockSpec(memory_space=pltpu.VMEM)
    hbm = pl.BlockSpec(memory_space=pltpu.HBM)
    shapes = (((block, hidden), bf16), ((block, width), bf16), ((width, hidden), f32))
    values = pl.pallas_call(
        functools.partial(kernel, rows, cols, sizes),
        out_shape=[pltpu.VMEM(*shape) for shape in shapes],
        in_specs=[hbm] * 7,
        out_specs=[vmem] * 3,
        scratch_shapes=scratch,
        compiler_params=pltpu.CompilerParams(
            collective_id=0, has_side_effects=True, vmem_limit_bytes=56 * 2**20),
    )(tile_counts, tile_rows[0], tile_cols[0], features, weight, cotangent, tile_values[0, 0])
    values = [pltpu.with_memory_space_constraint(value, pltpu.VMEM) for value in values]
    return pl.pallas_call(
        finish,
        out_shape=[jax.ShapeDtypeStruct(*shape) for shape in shapes],
        in_specs=[vmem] * 3,
        out_specs=[hbm] * 3,
        scratch_shapes=[dma((3,))],
    )(*values)


def solution(mesh):
    placed = (
        P(("row", "col"), None),
        P(),
        P(("row", "col"), None),
        P("row", "col", None, None, None),
        P("row", "col", None),
        P("row", "col", None),
        P("row", "col"),
    )
    return jax.shard_map(
        local,
        mesh=mesh,
        in_specs=placed,
        out_specs=(P(("row", "col"), None), P(("row", "col"), None), P()),
        check_vma=False,
    )
```
